128 devices in a mesh: expert: 32 (over y, x, core), tensor: 4 (over z).
Axes of the slice: x: 4, y: 4, z: 4, core: 2. Of those that a mesh axis runs over, the one named last changes fastest.
Arguments:
- tokens: bfloat16 [4096, 7168], P('expert', 'tensor'), may hold values from -6 to 6
- out_grad: bfloat16 [4096, 7168], P('expert', 'tensor'), may hold values from -6 to 6
- gate_weight: bfloat16 [32, 7168, 2048], P('expert', None, 'tensor'), may hold values from -0.0625 to 0.0625
- up_weight: bfloat16 [32, 7168, 2048], P('expert', None, 'tensor'), may hold values from -0.0625 to 0.0625
- proj_hidden: bfloat16 [2048, 64], P('tensor'), may hold values from -0.125 to 0.125
- proj_grad: bfloat16 [7168, 64], P('tensor'), may hold values from -0.0625 to 0.0625
- expert_ids: int32 [4096, 8], P('expert'), may hold values from 0 to 31, all different within a row; in each aligned block of 128 rows (0 to 127, 128 to 255, ...) at most 48 rows name the same one
- weight_index: int32 [4096, 8], P('expert'), may hold values from 0 to 63
- weight_table: float32 [64], replicated, may hold values from 0.02 to 0.4
- sequence_ids: int32 [4096], P('expert'), may hold values from 0 to 3, never falling along the last dimension, each value on 1 to 2048 neighbouring positions
Outputs:
- features: float32 [32, 4, 4096], P('expert', None, 'tensor')
The draws below stay inside these ranges and needn't reach their ends.
Inputs may be any that keep to these rules, and one draw needn't show every extreme that they name: `expert_ids`: within each aligned block of 128 tokens no expert is named by more than 48 tokens, a bound that some block reaches. `sequence_ids`: document ids never fall along the tokens; every document is present.
All inputs are finite; a program needn't handle non-finite values.
Results may differ from the reference program's by a relative error of at most 0.0029.
Values may be sent and summed in bfloat16 or wider, within the bound.
No kernel may reach another device: no remote copies, remote signals or barrier semaphores. Data moves between devices by JAX's collectives and lax.ppermute only.
A program may use at most 192 MiB of HBM per device.

```python
import math
import jax
import jax.numpy as jnp
import numpy as np
from jax import lax

D = 7168
FF = 2048
TOPK = 8
R = 64
SEQS = 4
LEVELS = 64
TOK_DEV = 128
EXPERTS = 32
TOKENS = 4096
CAP = 48
N_EXPERT = 32


def place_ends(result, rng, smallest, high):
    index_at = [jax.random.randint(jax.random.fold_in(rng, axis), (), 0, length) for axis, length in enumerate(result.shape)]
    longest = result.shape.index(max(result.shape))
    neighbour = index_at[:longest] + [(index_at[longest] + 1) % result.shape[longest]] + index_at[longest + 1:]
    return result.at[tuple(index_at)].set(smallest).at[tuple(neighbour)].set(high)


def levels(key, dims, shards, low, largest):
    level = 1.0
    for axis_at, blocks in shards:
        heights = jax.random.uniform(jax.random.fold_in(jax.random.fold_in(key, 6), axis_at), (blocks,), jnp.float32, low / len(shards), largest / len(shards))
        level = level * jnp.repeat(jnp.exp(heights), dims[axis_at] // blocks).reshape((-1,) + (1,) * (len(dims) - 1 - axis_at))
    return level


def split_up(number_of, total, bound, skew):
    portions = [(1 << 20) // math.isqrt(rank ** skew) + 1 for rank in range(2, number_of + 1)]
    spare, holding = total - bound - (number_of - 1), [1] * (number_of - 1)
    while spare > 0:
        free = [i for i in range(number_of - 1) if holding[i] < bound]
        mass, budget = sum([portions[i] for i in free]), spare
        for i in free:
            addition = min(bound - holding[i], max(1, budget * portions[i] // mass), spare)
            holding[i] = holding[i] + addition
            spare = spare - addition
    return np.array([bound] + holding)


def uneven_parts(rng, count, total, reach, lean):
    if count == 2:
        one = jax.random.randint(rng, (), max(1, total - reach), min(reach, total - 1) + 1)
        return jnp.stack([one, total - one])
    sizes = jnp.asarray(split_up(count, total, reach, lean), jnp.int32)
    couples = (count - 1) // 2
    giver, receiver = sizes[1:1 + 2 * couples:2], sizes[2:2 + 2 * couples:2]
    room = jnp.minimum(giver - 1, reach - receiver)
    passed = jax.random.randint(jax.random.fold_in(rng, 1), (couples,), 0, 1 << 20) % (room + 1)
    sizes = sizes.at[1:1 + 2 * couples:2].set(giver - passed).at[2:2 + 2 * couples:2].set(receiver + passed)
    return sizes[jax.random.permutation(jax.random.fold_in(rng, 2), count)]


def deal_out(stream_key, own, number, rows, count, top, most, skew):
    sequence = jax.random.permutation(stream_key, count)
    packed, ordinary = load_shares(count, rows * top, most, skew, True), load_shares(count, rows * top, most, skew, False)
    places = jnp.arange(count)

    def named(lengths, offset_by):
        used = int((lengths > 0).sum())
        fixed = max(1, used // 4)
        shifted = fixed + (places - fixed + offset_by * (used - fixed)) % max(1, count - fixed)
        return jnp.zeros((count,), jnp.int32).at[sequence[jnp.where(places < fixed, places, shifted)]].set(jnp.asarray(lengths, jnp.int32))

    lengths = jnp.where(number % 4 == 0, named(packed, number // 4), named(ordinary, number - number // 4 - 1))
    mixed = jax.random.permutation(jax.random.fold_in(own, 3), count)
    giver, taker = mixed[0:count // 2 * 2:2], mixed[1:count // 2 * 2:2]
    margin = jnp.minimum(lengths[giver] - 1, most - lengths[taker]) // 2
    margin = jnp.where((giver == sequence[0]) | (taker == sequence[0]) | (lengths[taker] == 0), 0, jnp.maximum(margin, 0))
    shifted = jax.random.randint(jax.random.fold_in(own, 4), (count // 2,), 0, 1 << 20) % (margin + 1)
    lengths = lengths.at[giver].add(-shifted).at[taker].add(shifted)
    items = jnp.searchsorted(jnp.cumsum(lengths), jnp.arange(rows * top), side="right").astype(jnp.int32)
    listing = items.reshape(top, rows).T
    listing = listing[jax.random.permutation(jax.random.fold_in(own, 1), rows)]
    offset_by = jax.random.randint(jax.random.fold_in(own, 2), (rows, 1), 0, top)
    return jnp.take_along_axis(listing, (jnp.arange(top)[None, :] + offset_by) % top, axis=1)


def load_shares(count, total, reach, lean, full):
    portions = [(1 << 20) // math.isqrt(standing ** lean) + 1 for standing in range(1, count + 1)]
    largest = reach if full else min(reach, max(-(-total // count), total * portions[0] // sum(portions)))
    least = 1 if total - largest >= count - 1 else 0
    counts, rest = [largest] + [least] * (count - 1), total - largest - least * (count - 1)
    while rest > 0:
        candidates = [i for i in range(1, count) if counts[i] < largest] or [i for i in range(1, count) if counts[i] < reach]
        mass, budget = sum([portions[i] for i in candidates]), rest
        for i in candidates:
            addition = min(reach - counts[i], max(1, budget * portions[i] // mass), rest)
            counts[i] = counts[i] + addition
            rest = rest - addition
    return np.array(counts)


def bell_draw(stream_key, extent, deviation, limit, split=(), held_as=jnp.bfloat16):
    array = deviation * jax.random.normal(stream_key, extent, jnp.float32)
    if split:
        array = array * levels(stream_key, extent, split, -0.22, 0.18)
    return jnp.clip(array, -limit, limit).astype(held_as)


def setup_inputs(seed: int = 0) -> dict:
    arg_keys = jax.random.split(jax.random.key(seed), 11)
    tokens = bell_draw(arg_keys[0], (TOKENS, D), 1.0, 6.0, ((0, 32), (1, 4)))
    out_grad = bell_draw(arg_keys[1], (TOKENS, D), 1.0, 6.0, ((0, 32), (1, 4)))
    gate_weight = bell_draw(arg_keys[2], (EXPERTS, D, FF), D ** -0.5, 0.0625, ((0, 32), (2, 4)))
    up_weight = bell_draw(arg_keys[3], (EXPERTS, D, FF), D ** -0.5, 0.0625, ((0, 32), (2, 4)))
    proj_hidden = bell_draw(arg_keys[4], (FF, R), FF ** -0.5, 0.125, ((0, 4),))
    proj_grad = bell_draw(arg_keys[5], (D, R), D ** -0.5, 0.0625, ((0, 4),))
    expert_ids_keys = jax.random.split(jax.random.fold_in(arg_keys[6], 1), TOKENS // TOK_DEV)
    expert_ids_turns = jax.random.permutation(jax.random.fold_in(arg_keys[6], 3), TOKENS // TOK_DEV)
    expert_ids = jax.vmap(lambda own, number: deal_out(jax.random.fold_in(arg_keys[6], 2), own, number, TOK_DEV, EXPERTS, TOPK, CAP, 2))(expert_ids_keys, expert_ids_turns).reshape((TOKENS, TOPK))
    weight_index = place_ends(jax.random.randint(arg_keys[7], (TOKENS, TOPK), 0, LEVELS), jax.random.fold_in(arg_keys[7], 1), 0, LEVELS - 1).astype(jnp.int32)
    weight_table = jnp.clip(jnp.exp(jax.random.uniform(arg_keys[8], (LEVELS,), jnp.float32, math.log(0.02), math.log(0.4))), 0.02, 0.4)
    sequence_ids = jnp.searchsorted(jnp.cumsum(uneven_parts(arg_keys[9], SEQS, TOKENS, 2 * TOKENS // SEQS, 1)), jnp.arange(TOKENS), side="right").astype(jnp.int32)
    return dict(tokens=tokens, out_grad=out_grad, gate_weight=gate_weight, up_weight=up_weight, proj_hidden=proj_hidden, proj_grad=proj_grad, expert_ids=expert_ids, weight_index=weight_index, weight_table=weight_table, sequence_ids=sequence_ids)


def reference(tokens, out_grad, gate_weight, up_weight, proj_hidden, proj_grad, expert_ids, weight_index, weight_table, sequence_ids):
    combine = weight_table[weight_index]
    right_all = jnp.dot(out_grad, proj_grad, preferred_element_type=jnp.float32)
    slots = N_EXPERT * CAP
    pad_tokens = jnp.concatenate([tokens, jnp.zeros((1, D), tokens.dtype)], axis=0)
    pad_right = jnp.concatenate([right_all, jnp.zeros((1, R), right_all.dtype)], axis=0)
    seq_hits = (sequence_ids[:, None] == jnp.arange(SEQS, dtype=jnp.int32)[None, :]).astype(jnp.float32)

    def one_expert(expert):
        hits = expert_ids == expert
        chosen = jnp.any(hits, axis=1)
        weight = jnp.sum(jnp.where(hits, combine, 0.0), axis=1)
        place = jnp.cumsum(chosen.astype(jnp.int32)) - 1
        place = jnp.where(chosen, place, slots).astype(jnp.int32)
        token_list = jnp.full((slots,), TOKENS, jnp.int32).at[place].set(jnp.arange(TOKENS, dtype=jnp.int32), mode="drop")
        rows = pad_tokens[token_list]
        gate_sum = jnp.dot(rows, gate_weight[expert], preferred_element_type=jnp.float32)
        up_sum = jnp.dot(rows, up_weight[expert], preferred_element_type=jnp.float32)
        hidden = (jax.nn.silu(gate_sum) * up_sum).astype(jnp.bfloat16)
        left = jnp.dot(hidden, proj_hidden, preferred_element_type=jnp.float32)
        seq_weight = seq_hits * weight[:, None]
        seq_weight = jnp.concatenate([seq_weight, jnp.zeros((1, SEQS), seq_weight.dtype)], axis=0)[token_list]
        right = pad_right[token_list]
        outer = jnp.einsum("ts,tr,tq->srq", seq_weight, left, right, precision=lax.Precision.HIGHEST)
        return outer.reshape(SEQS, R * R)

    return lax.map(one_expert, jnp.arange(EXPERTS, dtype=jnp.int32))
```

```python
import functools

import jax
import jax.numpy as jnp
from jax import lax
from jax.experimental import pallas as pl
from jax.experimental.pallas import tpu as pltpu
from jax.sharding import PartitionSpec as P

SEQS = 4
RING = 4
BOTH = ("expert", "tensor")

SOURCE = (0, -1, 1, 2)
TARGET = (0, 1, -1, 2)


def chip_pairs(dy, dx):
    return [
        (y * 8 + x * 2 + c, ((y + dy) % RING) * 8 + ((x + dx) % RING) * 2 + c)
        for y in range(RING)
        for x in range(RING)
        for c in range(2)
    ]


def z_pairs(step):
    return [(z, (z + step) % RING) for z in range(RING)]


def split_z_pairs(step):
    return [
        (e * RING + z, e * RING + (z + step * (1 - 2 * (e % 2))) % RING)
        for e in range(32)
        for z in range(RING)
    ]


def send(value, axis, step):
    if axis == "x":
        return lax.ppermute(value, "expert", chip_pairs(0, step))
    if axis == "y":
        return lax.ppermute(value, "expert", chip_pairs(step, 0))
    return lax.ppermute(value, "tensor", z_pairs(step))


def ring_gather(value, axis):
    return jnp.stack([value] + [send(value, axis, step) for step in TARGET[1:]])


def swap_cores(value):
    return lax.ppermute(value, "expert", [(e, e ^ 1) for e in range(32)])


def pick_kernel(dests, cap, slot_ref, own_ref, other_ref, *out_refs):
    def pick(data_ref):
        for b in range(RING):
            rows = data_ref[b]
            order = lax.broadcasted_iota(jnp.int32, (cap, rows.shape[0]), 0)
            hits = [
                jnp.where(slot_ref[b, d : d + 1, :] == order, 1.0, 0.0) for d in range(dests)
            ]
            hits = jnp.concatenate(hits, axis=0) if dests > 1 else hits[0]
            picked = jnp.dot(
                hits.astype(rows.dtype), rows, preferred_element_type=jnp.float32
            ).astype(rows.dtype)
            for d in range(dests):
                out_refs[d][b * cap : (b + 1) * cap, :] = picked[d * cap : (d + 1) * cap]

    pl.when(pl.program_id(0) == 0)(lambda: pick(own_ref))
    pl.when(pl.program_id(0) == 1)(lambda: pick(other_ref))


def pick_rows(kind, slots, own, other, cap):
    width = own.shape[-1]
    toks = own.shape[-2]
    dests = slots.shape[-2]
    hold_own = lambda h, i: jnp.where(h == 0, i, RING - 1)
    hold_other = lambda h, i: jnp.where(h == 0, 0, i)
    if kind == "rows":
        data = lambda hold: pl.BlockSpec(
            (None, RING, toks, width), lambda h, i: (hold(h, i), 0, 0, 0)
        )
        slot_spec = pl.BlockSpec((None, None, RING, dests, toks), lambda h, i: (h, i, 0, 0, 0))
        out_shape = (2, RING, RING * cap, width)
        out_spec = pl.BlockSpec((None, None, RING * cap, width), lambda h, i: (h, i, 0, 0))
    else:
        if kind == "outer":
            data = lambda hold: pl.BlockSpec(
                (None, RING, toks, width), lambda h, i: (hold(h, i), 0, 0, 0)
            )
        else:
            data = lambda hold: pl.BlockSpec(
                (RING, None, toks, width), lambda h, i: (0, hold(h, i), 0, 0)
            )
        slot_spec = pl.BlockSpec((None, RING, dests, toks), lambda h, i: (h, 0, 0, 0))
        out_shape = (2, RING * cap, RING * width)
        out_spec = pl.BlockSpec((None, RING * cap, width), lambda h, i: (h, 0, i))
    moved = 2 * own.size * 2 + dests * 2 * out_shape[-1] * out_shape[-2] * out_shape[-3]
    return pl.pallas_call(
        functools.partial(pick_kernel, dests, cap),
        grid=(2, RING),
        in_specs=[slot_spec, data(hold_own), data(hold_other)],
        out_specs=[out_spec] * dests,
        out_shape=[jax.ShapeDtypeStruct(out_shape, own.dtype)] * dests,
        compiler_params=pltpu.CompilerParams(vmem_limit_bytes=24 << 20),
        cost_estimate=pl.CostEstimate(
            flops=2 * 2 * own.size * cap * dests, bytes_accessed=moved, transcendentals=0
        ),
        name="pick_" + kind,
    )(slots, own, other)


def expert_kernel(plan, cap, place_ref, *refs):
    full, by_x, by_y, has_acc, last = plan
    refs = list(refs)
    take = lambda n: [refs.pop(0) for _ in range(n)]
    x_full, x_x, x_y = take(len(full)), take(len(by_x)), take(len(by_y))
    gate, up = take(2)
    acc_in = take(2) if has_acc else None
    proj = take(1)[0] if last else None
    outs = take(1 if last else 2)
    b_full, b_x, b_y, w_full, w_x, w_y, acc_g, acc_u, sems = take(9)
    c_full, c_part = b_full.shape[-1], w_x.shape[-2]
    start_x, start_y = c_full, c_full + c_part
    count = [0]

    def copy(src, dst):
        op = pltpu.make_async_copy(src, dst, sems.at[count[0]])
        count[0] += 1
        op.start()
        return op

    waits_full, waits_x, waits_y, waits_acc = [], [], [], []

    def fetch_full(p):
        z = place_ref[full[p]]
        waits_full.append(
            [copy(x_full[p], b_full.at[p])]
            + [
                copy(w.at[z, pl.ds(0, c_full)], w_full.at[p, n])
                for n, w in enumerate((gate, up))
            ]
        )

    def fetch_part(xs, buf, w_buf, start, waits):
        for p, x in enumerate(xs):
            ops = [copy(x, buf.at[p])]
            if p == 0:
                ops += [
                    copy(w.at[place_ref[r], pl.ds(start, c_part)], w_buf.at[n, r])
                    for n, w in enumerate((gate, up))
                    for r in range(RING)
                ]
            waits.append(ops)

    if full:
        fetch_full(0)
    if has_acc:
        waits_acc = [copy(acc_in[0], acc_g), copy(acc_in[1], acc_u)]
    for p in range(1, len(full)):
        fetch_full(p)
    fetch_part(x_x, b_x, w_x, start_x, waits_x)
    fetch_part(x_y, b_y, w_y, start_y, waits_y)

    width = acc_g.shape[-1]
    pair = 2 * RING * cap

    for p in range(len(full)):
        for op in waits_full[p]:
            op.wait()
        if p == 0:
            for op in waits_acc:
                op.wait()

        @pl.loop(0, 4)
        def _(m):
            h, half = m // 2, m % 2
            rows = b_full[p, h, pl.ds(2 * half, 2)].reshape(pair, c_full)
            for n, acc in enumerate((acc_g, acc_u)):
                view = acc.at[h, pl.ds(2 * half, 2)]
                got = jnp.dot(rows, w_full[p, n], preferred_element_type=jnp.float32)
                got = got.reshape(2, RING, cap, width)
                if p == 0 and not has_acc:
                    view[...] = got
                else:
                    view[...] += got

    def add_part(buf, w_buf, p, view_of):
        rows = buf[p].reshape(pair, RING * c_part)
        for n, acc in enumerate((acc_g, acc_u)):
            got = jnp.dot(
                rows,
                w_buf[n].reshape(RING * c_part, width),
                preferred_element_type=jnp.float32,
            )
            view_of(acc)[...] += got.reshape(2, RING, cap, width)

    for p, r in enumerate(by_x):
        for op in waits_x[p]:
            op.wait()
        add_part(b_x, w_x, p, lambda acc: acc.at[:, :, r])
    for p, r in enumerate(by_y):
        for op in waits_y[p]:
            op.wait()
        add_part(b_y, w_y, p, lambda acc: acc.at[:, r])

    if last:

        @pl.loop(0, 4)
        def _(m):
            h, half = m // 2, m % 2
            g = acc_g[h, pl.ds(2 * half, 2)].reshape(pair, width)
            u = acc_u[h, pl.ds(2 * half, 2)].reshape(pair, width)
            hidden = (g / (1.0 + jnp.exp(-g)) * u).astype(jnp.bfloat16)
            outs[0][pl.ds(pl.multiple_of(m * pair, pair), pair), :] = jnp.dot(
                hidden, proj[...], preferred_element_type=jnp.float32
            )
    else:
        ops = [copy(acc_g, outs[0]), copy(acc_u, outs[1])]
        for op in ops:
            op.wait()


def expert_step(name, place, full, by_x, by_y, gate, up, acc, proj, cap):
    last = proj is not None
    width = gate.shape[-1]
    c_full = full[0][1].shape[-1]
    c_part = by_x[0][1].shape[-1] // RING
    acc_type = jax.ShapeDtypeStruct((2, RING, RING, cap, width), jnp.float32)
    rows = 2 * RING * RING * cap
    hbm = pl.BlockSpec(memory_space=pl.ANY)
    vmem = pl.BlockSpec(memory_space=pltpu.VMEM)
    xs = [x for _, x in full] + [x for _, x in by_x] + [x for _, x in by_y]
    copies = 3 * len(full) + len(by_x) + len(by_y) + 4 * RING + 4
    plan = (
        tuple(i for i, _ in full),
        tuple(i for i, _ in by_x),
        tuple(i for i, _ in by_y),
        acc is not None,
        last,
    )
    bf = jnp.bfloat16
    return pl.pallas_call(
        functools.partial(expert_kernel, plan, cap),
        in_specs=[pl.BlockSpec(memory_space=pltpu.SMEM)]
        + [hbm] * (len(xs) + 2 + (2 if acc is not None else 0))
        + ([vmem] if last else []),
        out_specs=vmem if last else [hbm, hbm],
        out_shape=jax.ShapeDtypeStruct((rows, proj.shape[-1]), jnp.float32)
        if last
        else [acc_type, acc_type],
        scratch_shapes=[
            pltpu.VMEM((len(full), 2, RING, RING * cap, c_full), bf),
            pltpu.VMEM((len(by_x), 2, RING * cap, RING * c_part), bf),
            pltpu.VMEM((len(by_y), 2, RING * cap, RING * c_part), bf),
            pltpu.VMEM((len(full), 2, c_full, width), bf),
            pltpu.VMEM((2, RING, c_part, width), bf),
            pltpu.VMEM((2, RING, c_part, width), bf),
            pltpu.VMEM(acc_type.shape, jnp.float32),
            pltpu.VMEM(acc_type.shape, jnp.float32),
            pltpu.SemaphoreType.DMA((copies,)),
        ],
        compiler_params=pltpu.CompilerParams(vmem_limit_bytes=40 << 20),
        cost_estimate=pl.CostEstimate(
            flops=4 * width * sum(x.size for x in xs),
            bytes_accessed=2 * sum(x.size for x in xs) + 16 * gate.size,
            transcendentals=0,
        ),
        name=name,
    )(place, *xs, gate, up, *(acc or ()), *((proj,) if last else ()))


def local(
    tokens,
    out_grad,
    gate_weight,
    up_weight,
    proj_hidden,
    proj_grad,
    expert_ids,
    weight_index,
    weight_table,
    sequence_ids,
):
    experts = lax.axis_size("expert")
    toks, shard = tokens.shape
    topk = expert_ids.shape[1]
    cap = min(toks, 3 * toks * topk // (2 * experts))
    feats = proj_hidden.shape[-1]
    c_part = shard * 2 // 7 // 128 * 128
    c_full = shard - 2 * c_part
    e = lax.axis_index("expert")
    z = lax.axis_index("tensor")
    y, x, c = e // 8, (e // 2) % RING, e % 2
    source = jnp.array(SOURCE, jnp.int32)
    target = jnp.array(TARGET, jnp.int32)

    g0 = ring_gather(ring_gather(tokens[:, :c_full], "x"), "y")
    g1 = ring_gather(ring_gather(tokens[:, c_full : c_full + c_part], "y"), "z")
    g2 = ring_gather(ring_gather(tokens[:, c_full + c_part :], "z"), "x")

    ids_t = expert_ids.T
    note = jnp.concatenate(
        [ids_t, sequence_ids[None], jnp.zeros((7, toks), jnp.int32)], axis=0
    ).astype(jnp.bfloat16)
    notes = lax.all_to_all(
        jnp.broadcast_to(note[None], (experts,) + note.shape), "expert", 0, 0, tiled=True
    )
    by = (y + source) % RING
    bx = (x + source) % RING
    bc = jnp.stack([c, 1 - c])
    block = (by[None, :, None] * 8 + bx[None, None, :] * 2 + bc[:, None, None]).reshape(-1)
    notes = jnp.take(notes, block, axis=0, mode="clip").astype(jnp.int32)
    notes = notes.reshape(2, RING, RING, note.shape[0], toks)
    ids, seqs = notes[:, :, :, :topk], notes[:, :, :, topk]
    to_x = y * 8 + ((x + target) % RING) * 2 + c
    to_y = ((y + target) % RING) * 8 + x * 2 + c
    hit_own = jnp.any(ids == e, axis=3)
    hit_x = jnp.any(ids[:, :, 0, None] == to_x[None, None, :, None, None], axis=3)
    hit_y = jnp.any(ids[:, 0, :, None] == to_y[None, None, :, None, None], axis=3)
    every = jnp.arange(experts, dtype=jnp.int32)
    hits_src = ids_t[None] == every[:, None, None]
    hit_src = jnp.any(hits_src, axis=1)
    upto = (
        jnp.arange(toks, dtype=jnp.int32)[:, None] <= jnp.arange(toks, dtype=jnp.int32)[None, :]
    ).astype(jnp.bfloat16)

    def slots_of(hit):
        place = jnp.dot(
            hit.reshape(-1, toks).astype(jnp.bfloat16), upto, preferred_element_type=jnp.float32
        )
        return jnp.where(hit, place.reshape(hit.shape).astype(jnp.int32) - 1, -1)

    slot_own = slots_of(hit_own)
    slot_x = slots_of(hit_x)
    slot_y = slots_of(hit_y)
    slot_src = slots_of(hit_src)

    right_part = jnp.dot(out_grad, proj_grad, preferred_element_type=jnp.float32)
    right = jnp.sum(ring_gather(right_part, "z"), axis=0)
    levels = jnp.arange(weight_table.shape[0], dtype=jnp.int32)
    weights_t = jnp.sum(
        jnp.where(
            weight_index.T[:, :, None] == levels[None, None], weight_table[None, None], 0.0
        ),
        axis=2,
    )
    comb = jnp.sum(jnp.where(hits_src, weights_t[None], 0.0), axis=1)
    order = jnp.arange(cap, dtype=jnp.int32)
    spread = jnp.where(slot_src[:, None, :] == order[None, :, None], comb[:, None, :], 0.0)
    routed = jnp.dot(
        spread.reshape(experts * cap, toks), right, precision=lax.Precision.HIGHEST
    )
    high = lax.reduce_precision(routed, 8, 7)
    pieces = jnp.concatenate([high, routed - high], axis=1).astype(jnp.bfloat16)
    pieces = lax.all_to_all(
        pieces.reshape(experts, cap, 2 * feats), "expert", 0, 0, tiled=True
    )
    pieces = jnp.take(pieces, block, axis=0, mode="clip").astype(jnp.float32)
    routed = pieces[..., :feats] + pieces[..., feats:]
    slot_seq = jnp.sum(
        jnp.where(
            slot_own.reshape(experts, 1, toks) == order[None, :, None],
            seqs.reshape(experts, 1, toks),
            0,
        ),
        axis=2,
    )
    documents = jnp.arange(SEQS, dtype=jnp.int32)
    right_rows = jnp.where(
        slot_seq[:, :, None, None] == documents[None, None, :, None], routed[:, :, None, :], 0.0
    ).reshape(experts * cap, SEQS * feats)

    (p0,) = pick_rows("rows", slot_own[:, :, :, None], g0, swap_cores(g0), cap)
    p1 = pick_rows("outer", slot_x, g1, swap_cores(g1), cap)
    p2 = pick_rows("inner", slot_y, g2, swap_cores(g2), cap)
    near = lax.ppermute(p0, BOTH, split_z_pairs(1))
    other = lax.ppermute(p0, BOTH, split_z_pairs(-1))
    far = lax.ppermute(near, BOTH, split_z_pairs(1))
    q1 = [p1[0]] + [send(p1[d], "x", TARGET[d]) for d in (1, 2, 3)]
    q2 = [p2[0]] + [send(p2[d], "y", TARGET[d]) for d in (1, 2, 3)]

    way = 1 - 2 * c
    place = jnp.concatenate(
        [(z + source) % RING, jnp.stack([z, z - way, z + way, z + 2]) % RING]
    ).astype(jnp.int32)
    w_gate = gate_weight.reshape(RING, shard, -1)
    w_up = up_weight.reshape(RING, shard, -1)
    acc = expert_step(
        "expert_a", place, [(4, p0)], [(0, q1[0])], [(0, q2[0])], w_gate, w_up, None, None, cap
    )
    acc = expert_step(
        "expert_b",
        place,
        [(5, near), (6, other)],
        [(1, q1[1]), (2, q1[2])],
        [(1, q2[1]), (2, q2[2])],
        w_gate,
        w_up,
        acc,
        None,
        cap,
    )
    left = expert_step(
        "expert_c",
        place,
        [(7, far)],
        [(3, q1[3])],
        [(3, q2[3])],
        w_gate,
        w_up,
        acc,
        proj_hidden,
        cap,
    )

    outer = lax.dot_general(
        left, right_rows, (((0,), (0,)), ((), ())), precision=lax.Precision.HIGHEST
    )
    share = feats // RING
    mine = lambda k: lax.dynamic_slice_in_dim(outer, ((z + k) % RING) * share, share, 0)
    summed = mine(0)
    for k in (1, 2, 3):
        summed = summed + lax.ppermute(mine(k), "tensor", z_pairs(k))
    return summed.reshape(share, SEQS, feats).transpose(1, 0, 2).reshape(1, SEQS, share * feats)


def solution(mesh):
    placed = (
        P("expert", "tensor"),
        P("expert", "tensor"),
        P("expert", None, "tensor"),
        P("expert", None, "tensor"),
        P("tensor", None),
        P("tensor", None),
        P("expert", None),
        P("expert", None),
        P(),
        P("expert"),
    )
    return jax.shard_map(
        local, mesh=mesh, in_specs=placed, out_specs=P("expert", None, "tensor"), check_vma=False
    )
```

```python
import functools

import jax
import jax.numpy as jnp
from jax import lax
from jax.experimental import pallas as pl
from jax.experimental.pallas import tpu as pltpu
from jax.sharding import PartitionSpec as P


SEQS = 4
RING = 4
BOTH = ("expert", "tensor")

SOURCE = (0, -1, 1, 2)
TARGET = (0, 1, -1, 2)


def chip_pairs(dy, dx):
    return [
        (y * 8 + x * 2 + c, ((y + dy) % RING) * 8 + ((x + dx) % RING) * 2 + c)
        for y in range(RING)
        for x in range(RING)
        for c in range(2)
    ]


def z_pairs(step):
    return [(z, (z + step) % RING) for z in range(RING)]


def split_z_pairs(step):
    return [
        (e * RING + z, e * RING + (z + step * (1 - 2 * (e % 2))) % RING)
        for e in range(32)
        for z in range(RING)
    ]


def send(value, axis, step):
    if axis == "x":
        return lax.ppermute(value, "expert", chip_pairs(0, step))
    if axis == "y":
        return lax.ppermute(value, "expert", chip_pairs(step, 0))
    return lax.ppermute(value, "tensor", z_pairs(step))


def ring_pieces(value, axis):
    return [value] + [send(value, axis, step) for step in TARGET[1:]]


def swap_cores(value):
    return lax.ppermute(value, "expert", [(e, e ^ 1) for e in range(32)])


def pick_kernel(dests, cap, slot_ref, own_ref, other_ref, *out_refs):
    def pick(data_ref):
        for b in range(RING):
            rows = data_ref[b]
            order = lax.broadcasted_iota(jnp.int32, (cap, rows.shape[0]), 0)
            hits = [
                jnp.where(slot_ref[b, d : d + 1, :] == order, 1.0, 0.0) for d in range(dests)
            ]
            hits = jnp.concatenate(hits, axis=0) if dests > 1 else hits[0]
            picked = jnp.dot(
                hits.astype(rows.dtype), rows, preferred_element_type=jnp.float32
            ).astype(rows.dtype)
            for d in range(dests):
                out_refs[d][b * cap : (b + 1) * cap, :] = picked[d * cap : (d + 1) * cap]

    pl.when(pl.program_id(0) == 0)(lambda: pick(own_ref))
    pl.when(pl.program_id(0) == 1)(lambda: pick(other_ref))


def pick_rows(kind, slots, own, other, cap):
    width = own.shape[-1]
    toks = own.shape[-2]
    dests = slots.shape[-2]
    hold_own = lambda h, i: jnp.where(h == 0, i, RING - 1)
    hold_other = lambda h, i: jnp.where(h == 0, 0, i)
    if kind == "rows":
        data = lambda hold: pl.BlockSpec(
            (None, RING, toks, width), lambda h, i: (hold(h, i), 0, 0, 0)
        )
        slot_spec = pl.BlockSpec((None, None, RING, dests, toks), lambda h, i: (h, i, 0, 0, 0))
        out_shape = (2, RING, RING * cap, width)
        out_spec = pl.BlockSpec((None, None, RING * cap, width), lambda h, i: (h, i, 0, 0))
    else:
        if kind == "outer":
            data = lambda hold: pl.BlockSpec(
                (None, RING, toks, width), lambda h, i: (hold(h, i), 0, 0, 0)
            )
        else:
            data = lambda hold: pl.BlockSpec(
                (RING, None, toks, width), lambda h, i: (0, hold(h, i), 0, 0)
            )
        slot_spec = pl.BlockSpec((None, RING, dests, toks), lambda h, i: (h, 0, 0, 0))
        out_shape = (2, RING * cap, RING * width)
        out_spec = pl.BlockSpec((None, RING * cap, width), lambda h, i: (h, 0, i))
    moved = 2 * own.size * 2 + dests * 2 * out_shape[-1] * out_shape[-2] * out_shape[-3]
    return pl.pallas_call(
        functools.partial(pick_kernel, dests, cap),
        grid=(2, RING),
        in_specs=[slot_spec, data(hold_own), data(hold_other)],
        out_specs=[out_spec] * dests,
        out_shape=[pltpu.HBM(out_shape, own.dtype)] * dests,
        cost_estimate=pl.CostEstimate(
            flops=2 * 2 * own.size * cap * dests, bytes_accessed=moved, transcendentals=0
        ),
    )(slots, own, other)


def expert_kernel(plan, cap, place_ref, *refs):
    full, by_x, by_y, has_acc, last = plan
    refs = list(refs)
    take = lambda n: [refs.pop(0) for _ in range(n)]
    x_full, x_x, x_y = take(len(full)), take(len(by_x)), take(len(by_y))
    gate, up = take(2)
    acc_in = take(2) if has_acc else None
    proj = take(1)[0] if last else None
    outs = take(1 if last else 2)
    b_full, b_x, b_y, w_full, w_x, w_y, acc_g, acc_u, sems = take(9)
    c_full, c_part = b_full.shape[-1], w_x.shape[-2]
    start_x, start_y = c_full, c_full + c_part
    count = [0]

    def copy(src, dst):
        op = pltpu.make_async_copy(src, dst, sems.at[count[0]])
        count[0] += 1
        op.start()
        return op

    waits_full, waits_x, waits_y, waits_acc = [], [], [], []

    def fetch_full(p):
        z = place_ref[full[p]]
        waits_full.append(
            [copy(x_full[p], b_full.at[p])]
            + [
                copy(w.at[z, pl.ds(0, c_full)], w_full.at[p, n])
                for n, w in enumerate((gate, up))
            ]
        )

    def fetch_part(xs, buf, w_buf, start, waits):
        for p, x in enumerate(xs):
            ops = [copy(x, buf.at[p])]
            if p == 0:
                ops += [
                    copy(w.at[place_ref[r], pl.ds(start, c_part)], w_buf.at[n, r])
                    for n, w in enumerate((gate, up))
                    for r in range(RING)
                ]
            waits.append(ops)

    if full:
        fetch_full(0)
    if has_acc:
        waits_acc = [copy(acc_in[0], acc_g), copy(acc_in[1], acc_u)]
    for p in range(1, len(full)):
        fetch_full(p)
    fetch_part(x_x, b_x, w_x, start_x, waits_x)
    fetch_part(x_y, b_y, w_y, start_y, waits_y)

    width = acc_g.shape[-1]
    pair = 2 * RING * cap

    for p in range(len(full)):
        for op in waits_full[p]:
            op.wait()
        if p == 0:
            for op in waits_acc:
                op.wait()

        @pl.loop(0, 4)
        def _(m):
            h, half = m // 2, m % 2
            rows = b_full[p, h, pl.ds(2 * half, 2)].reshape(pair, c_full)
            for n, acc in enumerate((acc_g, acc_u)):
                view = acc.at[h, pl.ds(2 * half, 2)]
                got = jnp.dot(rows, w_full[p, n], preferred_element_type=jnp.float32)
                got = got.reshape(2, RING, cap, width)
                if p == 0 and not has_acc:
                    view[...] = got
                else:
                    view[...] += got

    def add_part(buf, w_buf, p, view_of):
        rows = buf[p].reshape(pair, RING * c_part)
        for n, acc in enumerate((acc_g, acc_u)):
            got = jnp.dot(
                rows,
                w_buf[n].reshape(RING * c_part, width),
                preferred_element_type=jnp.float32,
            )
            view_of(acc)[...] += got.reshape(2, RING, cap, width)

    for p, r in enumerate(by_x):
        for op in waits_x[p]:
            op.wait()
        add_part(b_x, w_x, p, lambda acc: acc.at[:, :, r])
    for p, r in enumerate(by_y):
        for op in waits_y[p]:
            op.wait()
        add_part(b_y, w_y, p, lambda acc: acc.at[:, r])

    if last:

        @pl.loop(0, 4)
        def _(m):
            h, half = m // 2, m % 2
            g = acc_g[h, pl.ds(2 * half, 2)].reshape(pair, width)
            u = acc_u[h, pl.ds(2 * half, 2)].reshape(pair, width)
            hidden = (g / (1.0 + jnp.exp(-g)) * u).astype(jnp.bfloat16)
            outs[0][pl.ds(pl.multiple_of(m * pair, pair), pair), :] = jnp.dot(
                hidden, proj[...], preferred_element_type=jnp.float32
            )
    else:
        ops = [copy(acc_g, outs[0]), copy(acc_u, outs[1])]
        for op in ops:
            op.wait()


def expert_step(place, full, by_x, by_y, gate, up, acc, proj, cap):
    last = proj is not None
    width = gate.shape[-1]
    c_full = full[0][1].shape[-1]
    c_part = by_x[0][1].shape[-1] // RING
    acc_type = jax.ShapeDtypeStruct((2, RING, RING, cap, width), jnp.float32)
    rows = 2 * RING * RING * cap
    hbm = pl.BlockSpec(memory_space=pltpu.HBM)
    vmem = pl.BlockSpec(memory_space=pltpu.VMEM)
    xs = [x for _, x in full] + [x for _, x in by_x] + [x for _, x in by_y]
    copies = 3 * len(full) + len(by_x) + len(by_y) + 4 * RING + 4
    plan = (
        tuple(i for i, _ in full),
        tuple(i for i, _ in by_x),
        tuple(i for i, _ in by_y),
        acc is not None,
        last,
    )
    bf = jnp.bfloat16
    return pl.pallas_call(
        functools.partial(expert_kernel, plan, cap),
        in_specs=[pl.BlockSpec(memory_space=pltpu.SMEM)]
        + [hbm] * (len(xs) + 2 + (2 if acc is not None else 0))
        + ([vmem] if last else []),
        out_specs=vmem if last else [hbm, hbm],
        out_shape=jax.ShapeDtypeStruct((rows, proj.shape[-1]), jnp.float32)
        if last
        else [pltpu.HBM(acc_type.shape, jnp.float32)] * 2,
        scratch_shapes=[
            pltpu.VMEM((len(full), 2, RING, RING * cap, c_full), bf),
            pltpu.VMEM((len(by_x), 2, RING * cap, RING * c_part), bf),
            pltpu.VMEM((len(by_y), 2, RING * cap, RING * c_part), bf),
            pltpu.VMEM((len(full), 2, c_full, width), bf),
            pltpu.VMEM((2, RING, c_part, width), bf),
            pltpu.VMEM((2, RING, c_part, width), bf),
            pltpu.VMEM(acc_type.shape, jnp.float32),
            pltpu.VMEM(acc_type.shape, jnp.float32),
            pltpu.SemaphoreType.DMA((copies,)),
        ],
        cost_estimate=pl.CostEstimate(
            flops=4 * width * sum(x.size for x in xs),
            bytes_accessed=2 * sum(x.size for x in xs) + 16 * gate.size,
            transcendentals=0,
        ),
    )(place, *xs, gate, up, *(acc or ()), *((proj,) if last else ()))


def local(
    tokens,
    out_grad,
    gate_weight,
    up_weight,
    proj_hidden,
    proj_grad,
    expert_ids,
    weight_index,
    weight_table,
    sequence_ids,
):
    experts = lax.axis_size("expert")
    toks, shard = tokens.shape
    topk = expert_ids.shape[1]
    cap = min(toks, 3 * toks * topk // (2 * experts))
    feats = proj_hidden.shape[-1]
    c_part = shard * 2 // 7 // 128 * 128
    c_full = shard - 2 * c_part
    e = lax.axis_index("expert")
    z = lax.axis_index("tensor")
    y, x, c = e // 8, (e // 2) % RING, e % 2
    source = jnp.array(SOURCE, jnp.int32)
    target = jnp.array(TARGET, jnp.int32)

    t0 = ring_pieces(tokens[:, :c_full], "x")
    t1 = ring_pieces(tokens[:, c_full : c_full + c_part], "y")
    t2 = ring_pieces(tokens[:, c_full + c_part :], "z")
    right_part = jnp.dot(out_grad, proj_grad, preferred_element_type=jnp.float32)
    ids_t = expert_ids.T
    note = jnp.concatenate(
        [ids_t, sequence_ids[None], jnp.zeros((7, toks), jnp.int32)], axis=0
    ).astype(jnp.bfloat16)
    notes = jnp.broadcast_to(note[None], (experts,) + note.shape)
    t0, t1, t2, right_part, notes = lax.optimization_barrier((t0, t1, t2, right_part, notes))
    t0 = ring_pieces(jnp.stack(t0), "y")
    t1 = ring_pieces(jnp.stack(t1), "z")
    t2 = ring_pieces(jnp.stack(t2), "x")
    rights = ring_pieces(right_part, "z")
    notes = lax.all_to_all(notes, "expert", 0, 0, tiled=True)
    by = (y + source) % RING
    bx = (x + source) % RING
    bc = jnp.stack([c, 1 - c])
    block = (by[None, :, None] * 8 + bx[None, None, :] * 2 + bc[:, None, None]).reshape(-1)
    notes = jnp.take(notes, block, axis=0, mode="clip").astype(jnp.int32)
    notes = notes.reshape(2, RING, RING, note.shape[0], toks)
    ids, seqs = notes[:, :, :, :topk], notes[:, :, :, topk]
    to_x = y * 8 + ((x + target) % RING) * 2 + c
    to_y = ((y + target) % RING) * 8 + x * 2 + c
    hit_own = jnp.any(ids == e, axis=3)
    hit_x = jnp.any(ids[:, :, 0, None] == to_x[None, None, :, None, None], axis=3)
    hit_y = jnp.any(ids[:, 0, :, None] == to_y[None, None, :, None, None], axis=3)
    every = jnp.arange(experts, dtype=jnp.int32)
    hits_src = ids_t[None] == every[:, None, None]
    hit_src = jnp.any(hits_src, axis=1)
    upto = (
        jnp.arange(toks, dtype=jnp.int32)[:, None] <= jnp.arange(toks, dtype=jnp.int32)[None, :]
    ).astype(jnp.bfloat16)

    def slots_of(hit):
        place = jnp.dot(
            hit.reshape(-1, toks).astype(jnp.bfloat16), upto, preferred_element_type=jnp.float32
        )
        return jnp.where(hit, place.reshape(hit.shape).astype(jnp.int32) - 1, -1)

    slot_own = slots_of(hit_own)
    slot_x = slots_of(hit_x)
    slot_y = slots_of(hit_y)
    slot_src = slots_of(hit_src)

    right = rights[0] + rights[1] + rights[2] + rights[3]
    levels = jnp.arange(weight_table.shape[0], dtype=jnp.int32)
    weights_t = jnp.sum(
        jnp.where(
            weight_index.T[:, :, None] == levels[None, None], weight_table[None, None], 0.0
        ),
        axis=2,
    )
    comb = jnp.sum(jnp.where(hits_src, weights_t[None], 0.0), axis=1)
    order = jnp.arange(cap, dtype=jnp.int32)
    spread = jnp.where(slot_src[:, None, :] == order[None, :, None], comb[:, None, :], 0.0)
    t0, t1, t2, spread, right, slot_own, slot_x, slot_y = lax.optimization_barrier(
        (t0, t1, t2, spread, right, slot_own, slot_x, slot_y)
    )
    routed = jnp.dot(
        spread.reshape(experts * cap, toks), right, precision=lax.Precision.HIGHEST
    )
    high = lax.reduce_precision(routed, 8, 7)
    pieces = jnp.concatenate([high, routed - high], axis=1).astype(jnp.bfloat16)
    pieces = lax.all_to_all(
        pieces.reshape(experts, cap, 2 * feats), "expert", 0, 0, tiled=True
    )
    pieces = jnp.take(pieces, block, axis=0, mode="clip").astype(jnp.float32)
    routed = pieces[..., :feats] + pieces[..., feats:]
    slot_seq = jnp.sum(
        jnp.where(
            slot_own.reshape(experts, 1, toks) == order[None, :, None],
            seqs.reshape(experts, 1, toks),
            0,
        ),
        axis=2,
    )
    routed = routed.reshape(experts * cap, feats)
    slot_seq = slot_seq.reshape(experts * cap, 1)
    right_rows = jnp.concatenate(
        [jnp.where(slot_seq == s, routed, 0.0) for s in range(SEQS)], axis=1
    )

    g0, g1, g2 = jnp.stack(t0), jnp.stack(t1), jnp.stack(t2)
    h0 = swap_cores(g0)
    h1 = swap_cores(g1)
    h2 = swap_cores(g2)
    (p0,) = pick_rows("rows", slot_own[:, :, :, None], g0, h0, cap)
    p1 = pick_rows("outer", slot_x, g1, h1, cap)
    p2 = pick_rows("inner", slot_y, g2, h2, cap)
    near = lax.ppermute(p0, BOTH, split_z_pairs(1))
    other = lax.ppermute(p0, BOTH, split_z_pairs(-1))
    far = lax.ppermute(near, BOTH, split_z_pairs(1))
    q1, q2 = [p1[0]], [p2[0]]
    for d in (1, 2, 3):
        q1.append(send(p1[d], "x", TARGET[d]))
        q2.append(send(p2[d], "y", TARGET[d]))

    way = 1 - 2 * c
    place = jnp.concatenate(
        [(z + source) % RING, jnp.stack([z, z - way, z + way, z + 2]) % RING]
    ).astype(jnp.int32)
    w_gate = gate_weight.reshape(RING, shard, -1)
    w_up = up_weight.reshape(RING, shard, -1)
    acc = expert_step(place, [(4, p0)], [(0, q1[0])], [(0, q2[0])], w_gate, w_up, None, None, cap)
    acc = expert_step(
        place,
        [(5, near), (6, other)],
        [(1, q1[1]), (2, q1[2])],
        [(1, q2[1]), (2, q2[2])],
        w_gate,
        w_up,
        acc,
        None,
        cap,
    )
    left = expert_step(
        place, [(7, far)], [(3, q1[3])], [(3, q2[3])], w_gate, w_up, acc, proj_hidden, cap
    )

    outer = lax.dot_general(
        left, right_rows, (((0,), (0,)), ((), ())), precision=lax.Precision.HIGHEST
    )
    share = feats // RING
    mine = lambda k: lax.dynamic_slice_in_dim(outer, ((z + k) % RING) * share, share, 0)
    summed = mine(0)
    for k in (1, 2, 3):
        summed = summed + lax.ppermute(mine(k), "tensor", z_pairs(k))
    return summed.reshape(share, SEQS, feats).transpose(1, 0, 2).reshape(1, SEQS, share * feats)


def solution(mesh):
    placed = (
        P("expert", "tensor"),
        P("expert", "tensor"),
        P("expert", None, "tensor"),
        P("expert", None, "tensor"),
        P("tensor", None),
        P("tensor", None),
        P("expert", None),
        P("expert", None),
        P(),
        P("expert"),
    )
    return jax.shard_map(
        local, mesh=mesh, in_specs=placed, out_specs=P("expert", None, "tensor"), check_vma=False
    )
```

```python
import functools

import jax
import jax.numpy as jnp
from jax import lax
from jax.experimental import pallas as pl
from jax.experimental.pallas import tpu as pltpu
from jax.sharding import PartitionSpec as P


SEQS = 4
RING = 4
BOTH = ("expert", "tensor")

SOURCE = (0, -1, 1, 2)
TARGET = (0, 1, -1, 2)


def chip_pairs(dy, dx):
    return [
        (y * 8 + x * 2 + c, ((y + dy) % RING) * 8 + ((x + dx) % RING) * 2 + c)
        for y in range(RING)
        for x in range(RING)
        for c in range(2)
    ]


def z_pairs(step):
    return [(z, (z + step) % RING) for z in range(RING)]


def split_z_pairs(step):
    return [
        (e * RING + z, e * RING + (z + step * (1 - 2 * (e % 2))) % RING)
        for e in range(32)
        for z in range(RING)
    ]


def send(value, axis, step):
    if axis == "x":
        return lax.ppermute(value, "expert", chip_pairs(0, step))
    if axis == "y":
        return lax.ppermute(value, "expert", chip_pairs(step, 0))
    return lax.ppermute(value, "tensor", z_pairs(step))


def ring_pieces(value, axis):
    return [value] + [send(value, axis, step) for step in TARGET[1:]]


def expert_kernel(plan, place_ref, *refs):
    pieces, has_acc, last = plan
    refs = list(refs)
    take = lambda n: [refs.pop(0) for _ in range(n)]
    xs = take(len(pieces))
    gate, up = take(2)
    acc_in = take(2) if has_acc else None
    proj = take(1)[0] if last else None
    outs = take(1 if last else 2)
    x_bufs = take(len(pieces))
    w_bufs = take(len(pieces))
    acc_g, acc_u, sems = take(3)
    count = [0]

    def copy(src, dst):
        op = pltpu.make_async_copy(src, dst, sems.at[count[0]])
        count[0] += 1
        op.start()
        return op

    waits = []
    for p, segments in enumerate(pieces):
        ops = [copy(xs[p].at[:, pl.ds(0, x_bufs[p].shape[1])], x_bufs[p])]
        at = 0
        for z_at, row, width in segments:
            for n, w in enumerate((gate, up)):
                ops.append(
                    copy(
                        w.at[place_ref[z_at], pl.ds(row, width)],
                        w_bufs[p].at[n, pl.ds(at, width)],
                    )
                )
            at += width
        if p == 0 and has_acc:
            ops += [copy(acc_in[0], acc_g), copy(acc_in[1], acc_u)]
        waits.append(ops)

    rows = acc_g.shape[0]
    part = rows // 4
    for p in range(len(pieces)):
        for op in waits[p]:
            op.wait()

        @pl.loop(0, 4)
        def _(m):
            at = pl.ds(pl.multiple_of(m * part, part), part)
            x = x_bufs[p][at, :]
            for n, acc in enumerate((acc_g, acc_u)):
                got = jnp.dot(x, w_bufs[p][n], preferred_element_type=jnp.float32)
                if p == 0 and not has_acc:
                    acc[at, :] = got
                else:
                    acc[at, :] += got

    if last:

        @pl.loop(0, 4)
        def _(m):
            at = pl.ds(pl.multiple_of(m * part, part), part)
            g = acc_g[at, :]
            hidden = (g / (1.0 + jnp.exp(-g)) * acc_u[at, :]).astype(jnp.bfloat16)
            outs[0][at, :] = jnp.dot(hidden, proj[...], preferred_element_type=jnp.float32)
    else:
        ops = [copy(acc_g, outs[0]), copy(acc_u, outs[1])]
        for op in ops:
            op.wait()


def expert_step(place, pieces, gate, up, acc, proj):
    last = proj is not None
    width = gate.shape[-1]
    xs = [x for x, _ in pieces]
    plan = (tuple(tuple(segs) for _, segs in pieces), acc is not None, last)
    rows = xs[0].shape[0]
    depths = [sum(width for _, _, width in segs) for _, segs in pieces]
    hbm = pl.BlockSpec(memory_space=pltpu.HBM)
    vmem = pl.BlockSpec(memory_space=pltpu.VMEM)
    copies = sum(1 + 2 * len(segs) for _, segs in pieces) + 4
    bf = jnp.bfloat16
    return pl.pallas_call(
        functools.partial(expert_kernel, plan),
        in_specs=[pl.BlockSpec(memory_space=pltpu.SMEM)]
        + [hbm] * (len(xs) + 2 + (2 if acc is not None else 0))
        + ([vmem] if last else []),
        out_specs=vmem if last else [hbm, hbm],
        out_shape=jax.ShapeDtypeStruct((rows, proj.shape[-1]), jnp.float32)
        if last
        else [pltpu.HBM((rows, width), jnp.float32)] * 2,
        scratch_shapes=[pltpu.VMEM((rows, d), bf) for d in depths]
        + [pltpu.VMEM((2, d, width), bf) for d in depths]
        + [
            pltpu.VMEM((rows, width), jnp.float32),
            pltpu.VMEM((rows, width), jnp.float32),
            pltpu.SemaphoreType.DMA((copies,)),
        ],
        cost_estimate=pl.CostEstimate(
            flops=4 * width * rows * sum(depths),
            bytes_accessed=(2 * rows + 4 * width) * sum(depths) + 16 * rows * width,
            transcendentals=0,
        ),
    )(place, *xs, gate, up, *(acc or ()), *((proj,) if last else ()))


def relay(value):
    near = lax.ppermute(value, BOTH, split_z_pairs(1))
    other = lax.ppermute(value, BOTH, split_z_pairs(-1))
    far = lax.ppermute(near, BOTH, split_z_pairs(1))
    return near, other, far


def local(
    tokens,
    out_grad,
    gate_weight,
    up_weight,
    proj_hidden,
    proj_grad,
    expert_ids,
    weight_index,
    weight_table,
    sequence_ids,
):
    experts = lax.axis_size("expert")
    toks, shard = tokens.shape
    topk = expert_ids.shape[1]
    cap = min(toks, 3 * toks * topk // (2 * experts))
    slots = experts * cap
    feats = proj_hidden.shape[-1]
    c_d = shard * 2 // 7 // 128 * 128
    c_1 = (shard - c_d) // 2 // 128 * 128
    c_2 = shard - c_d - c_1
    e = lax.axis_index("expert")
    z = lax.axis_index("tensor")
    c = e % 2
    bf = jnp.bfloat16

    ids_t = expert_ids.T
    every = jnp.arange(experts, dtype=jnp.int32)
    hits = ids_t[None] == every[:, None, None]
    hit = jnp.any(hits, axis=1)
    index = jnp.arange(toks, dtype=jnp.int32)
    upto = (index[:, None] <= index[None, :]).astype(bf)
    count = jnp.dot(hit.astype(bf), upto, preferred_element_type=jnp.float32)
    slot = jnp.where(hit, count.astype(jnp.int32) - 1, -1)
    order = jnp.arange(cap, dtype=jnp.int32)
    chosen = slot[:, None, :] == order[None, :, None]
    picks = jnp.where(chosen, 1.0, 0.0).astype(bf).reshape(slots, toks)

    def pick(value):
        return jnp.dot(picks, value, preferred_element_type=jnp.float32).astype(bf)

    def exchange(value):
        value = lax.all_to_all(
            value.reshape(experts, cap, -1), "expert", 0, 0, tiled=True
        )
        return value.reshape(slots, -1)

    d_parts = ring_pieces(tokens[:, c_1 + c_2 :], "z")
    x1 = exchange(pick(tokens[:, :c_1]))
    x2 = pick(tokens[:, c_1 : c_1 + c_2])

    right_part = jnp.dot(out_grad, proj_grad, preferred_element_type=jnp.float32)
    rights = ring_pieces(right_part, "z")
    right = rights[0] + rights[1] + rights[2] + rights[3]
    levels = jnp.arange(weight_table.shape[0], dtype=jnp.int32)
    weights_t = jnp.sum(
        jnp.where(
            weight_index.T[:, :, None] == levels[None, None], weight_table[None, None], 0.0
        ),
        axis=2,
    )
    comb = jnp.sum(jnp.where(hits, weights_t[None], 0.0), axis=1)
    spread = jnp.where(chosen, comb[:, None, :], 0.0).reshape(slots, toks)
    routed = jnp.dot(spread, right, precision=lax.Precision.HIGHEST)
    documents = pick(jnp.broadcast_to(sequence_ids.astype(bf)[:, None], (toks, feats)))
    high = lax.reduce_precision(routed, 8, 7)
    rest = routed - high
    middle = lax.reduce_precision(rest, 8, 7)
    terms = jnp.concatenate([high, middle, rest - middle], axis=1).astype(bf)
    d_rows = pick(jnp.concatenate(d_parts, axis=1))
    d_sent = jnp.concatenate([d_rows, terms, documents], axis=1)
    x2, d_sent = lax.optimization_barrier((x2, d_sent))
    x2 = exchange(x2)
    d_got = exchange(d_sent)
    side = d_got[:, RING * c_d :].astype(jnp.float32)
    routed = side[:, :feats] + side[:, feats : 2 * feats] + side[:, 2 * feats : 3 * feats]
    slot_seq = side[:, 3 * feats : 3 * feats + 1]
    right_rows = jnp.concatenate(
        [jnp.where(slot_seq == s, routed, 0.0) for s in range(SEQS)], axis=1
    )

    near1, other1, far1 = relay(x1)
    near2, other2, far2 = relay(x2)
    way = 1 - 2 * c
    source = jnp.array(SOURCE, jnp.int32)
    place = jnp.concatenate(
        [(z + source) % RING, jnp.stack([z, z - way, z + way, z + 2]) % RING]
    ).astype(jnp.int32)
    w_gate = gate_weight.reshape(RING, shard, -1)
    w_up = up_weight.reshape(RING, shard, -1)
    one = lambda x, at: (x, [(at, 0, c_1)])
    two = lambda x, at: (x, [(at, c_1, c_2)])
    seg_d = [(r, c_1 + c_2, c_d) for r in range(RING)]
    acc = expert_step(place, [one(x1, 4), two(x2, 4)], w_gate, w_up, None, None)
    acc = expert_step(place, [one(near1, 5), one(other1, 6), one(far1, 7)], w_gate, w_up, acc, None)
    acc = expert_step(place, [two(near2, 5), two(other2, 6), two(far2, 7)], w_gate, w_up, acc, None)
    left = expert_step(place, [(d_got, seg_d)], w_gate, w_up, acc, proj_hidden)

    outer = lax.dot_general(
        left, right_rows, (((0,), (0,)), ((), ())), precision=lax.Precision.HIGHEST
    )
    share = feats // RING
    mine = lambda k: lax.dynamic_slice_in_dim(outer, ((z + k) % RING) * share, share, 0)
    summed = mine(0)
    for k in (1, 2, 3):
        summed = summed + lax.ppermute(mine(k), "tensor", z_pairs(k))
    return summed.reshape(share, SEQS, feats).transpose(1, 0, 2).reshape(1, SEQS, share * feats)


def solution(mesh):
    placed = (
        P("expert", "tensor"),
        P("expert", "tensor"),
        P("expert", None, "tensor"),
        P("expert", None, "tensor"),
        P("tensor", None),
        P("tensor", None),
        P("expert", None),
        P("expert", None),
        P(),
        P("expert"),
    )
    return jax.shard_map(
        local, mesh=mesh, in_specs=placed, out_specs=P("expert", None, "tensor"), check_vma=False
    )
```
